32 devices in a mesh: seg: 2 (over y), chan: 8 (over z, x), band: 2 (over core).
Axes of the slice: x: 2, y: 2, z: 4, core: 2. Of those that a mesh axis runs over, the one named last changes fastest.
Arguments:
- strain: float32 [2048, 8, 3000], P(('seg', 'chan'), 'band'), parts along dimension 0, may hold values from -84 to 84
- offsets: int32 [16, 6], P(('seg', 'band')), parts along dimension 0, may hold values from 0 to 2000, as said below
- bins: int32 [256], replicated, may hold values from 1 to 499, as said below
Outputs:
- cross_spectra: bfloat16 [2048, 1024, 2, 256], P(('seg', 'chan'), None, None, 'band'), parts along dimension 0
The draws below stay inside these ranges and needn't reach their ends.
There are 2 independent parts, one for each index of `seg`. The reference program is written for one: setup_inputs(seed, part) draws one part's arguments, and reference() takes and returns one part's arrays. A program takes and returns all parts, laid end to end along the dimension named above; an argument that names none is the same for every part. Nothing has to cross between parts.
Inputs may be any that keep to these rules, and one draw needn't show every extreme that they name: `offsets`: each window lies inside its minute file. `bins`: ascending and distinct.
All inputs are finite; a program needn't handle non-finite values.
Results may differ from the reference program's by a relative error of at most 0.0062.
Values may be sent and summed in bfloat16 or wider, within the bound.
A program may use at most 320 MiB of HBM per device.

```python
import math
import jax
import jax.numpy as jnp
from jax import lax

CHANNELS = 1024
SAMPLES = 3000
WIN_LEN = 1000
WIN_FILE = 6
BINS = 256
GROUP = 128
REACH = 64
FILES = 8


def draw_strain(key, part):
    key_noise, key_color, key_envelope = jax.random.split(key, 3)
    noise_vals = jnp.clip(jax.random.normal(key_noise, (CHANNELS, FILES, SAMPLES + 1), jnp.float32), -4.0, 4.0)
    low_edge = 0.3
    high_edge = 3.0
    color_gain = jnp.exp(jax.random.uniform(key_color, (CHANNELS, 1, 1), jnp.float32, math.log(low_edge), math.log(high_edge)))
    envelope = jnp.exp(jax.random.uniform(key_envelope, (CHANNELS, FILES, SAMPLES // 100, 1), jnp.float32, math.log(0.3), math.log(3.0)))
    envelope = jnp.broadcast_to(envelope, (CHANNELS, FILES, SAMPLES // 100, 100)).reshape(CHANNELS, FILES, SAMPLES)
    current = noise_vals[:, :, 1:]
    previous = noise_vals[:, :, :-1]
    return (current + color_gain * (current - previous)) * envelope


def draw_offsets(key, part):
    key_values, key_lowpos, key_highpos = jax.random.split(key, 3)
    entries = FILES * WIN_FILE
    values = jax.random.randint(key_values, (entries,), 0, SAMPLES - WIN_LEN + 1, jnp.int32)
    low_pos = jax.random.randint(key_lowpos, (), 0, entries // 2, jnp.int32)
    high_pos = jax.random.randint(key_highpos, (), entries // 2, entries, jnp.int32)
    values = values.at[low_pos].set(0).at[high_pos].set(SAMPLES - WIN_LEN)
    return values.reshape(FILES, WIN_FILE)


def draw_bins(key, part):
    shuffled = jax.random.permutation(key, WIN_LEN // 2 - 3) + 2
    chosen = jnp.sort(shuffled[:BINS - 2]).astype(jnp.int32)
    first_bin = jnp.array([1], jnp.int32)
    last_bin = jnp.array([WIN_LEN // 2 - 1], jnp.int32)
    return jnp.concatenate([first_bin, chosen, last_bin])


def setup_inputs(seed: int = 0, part: int = 0) -> dict:
    arg_keys = jax.random.split(jax.random.key(seed), 4)
    own_keys = jax.random.split(jax.random.fold_in(arg_keys[3], part), 4)
    strain = draw_strain(jax.random.fold_in(jax.random.fold_in(arg_keys[3], part), 71), part)
    offsets = draw_offsets(jax.random.fold_in(jax.random.fold_in(arg_keys[3], part), 71), part)
    bins = draw_bins(jax.random.fold_in(arg_keys[3], 71), part)
    return dict(strain=strain, offsets=offsets, bins=bins)


def normalize(strain):
    width = 2 * REACH + 1
    magnitude = jnp.abs(strain)
    zero_val = jnp.zeros((), magnitude.dtype)
    running = lax.reduce_window(magnitude, zero_val, lax.add, (1, 1, width), (1, 1, 1), ((0, 0), (0, 0), (REACH, REACH)))
    unit_row = jnp.ones((strain.shape[2],), magnitude.dtype)
    counts = lax.reduce_window(unit_row, zero_val, lax.add, (width,), (1,), ((REACH, REACH),))
    return strain / (running / counts + 1e-06)

def cut_windows(normed, offsets):

    def one_file(rows, starts):
        return jax.vmap(lambda start_pos: lax.dynamic_slice_in_dim(rows, start_pos, WIN_LEN, 1))(starts)
    pieces = jax.vmap(one_file, in_axes=(1, 0))(normed, offsets.astype(jnp.int32))
    sample_pos = jnp.arange(WIN_LEN, dtype=jnp.float32)
    hann_taper = 0.5 - 0.5 * jnp.cos(2.0 * math.pi * (sample_pos + 0.5) / WIN_LEN)
    return (jnp.transpose(pieces, (2, 0, 1, 3)) * hann_taper).astype(jnp.bfloat16)

def make_table(bins):
    sample_idx = jnp.arange(WIN_LEN, dtype=jnp.int32)
    phase_idx = sample_idx[:, None] * bins.astype(jnp.int32)[None, :] % WIN_LEN
    angles = phase_idx.astype(jnp.float32) * (2.0 * math.pi / WIN_LEN)
    return jnp.concatenate([jnp.cos(angles), -jnp.sin(angles)], axis=1).astype(jnp.bfloat16)

def spectra(windows, table):
    flat_rows = windows.reshape(-1, WIN_LEN)
    result = jnp.dot(flat_rows, table, preferred_element_type=jnp.float32)
    return result.reshape(windows.shape[0], windows.shape[1] * windows.shape[2], 2, table.shape[1] // 2)

def whiten(spec):
    chan_rows, win_count, _, bin_count = spec.shape
    grouped = spec.reshape(chan_rows, win_count, 2, bin_count // GROUP, GROUP)
    power_mean = lax.optimization_barrier(jnp.mean(lax.optimization_barrier(jnp.sum(grouped * grouped, axis=2)), axis=-1, keepdims=True))
    gain_inv = lax.rsqrt(power_mean + 1e-06)[:, :, None]
    return (grouped * gain_inv).reshape(spec.shape).astype(jnp.bfloat16)

def reference(strain, offsets, bins):
    normed = normalize(strain)
    windows = cut_windows(normed, offsets)
    whitened = whiten(spectra(windows, make_table(bins)))
    whole_u = whitened.astype(jnp.float32)
    whole_v = jnp.stack([whole_u[:, :, 1], -whole_u[:, :, 0]], axis=2)
    win_count = whole_u.shape[1]
    block_rows = 64
    u_blocks = whole_u.reshape((-1, block_rows) + whole_u.shape[1:])
    v_blocks = whole_v.reshape((-1, block_rows) + whole_v.shape[1:])

    def one_block(operands):
        u_block, v_block = operands
        real_part = jnp.einsum('iwcf,jwcf->ijf', u_block, whole_u)
        imag_part = jnp.einsum('iwcf,jwcf->ijf', v_block, whole_u)
        return (jnp.stack([real_part, imag_part], axis=2) / win_count).astype(jnp.bfloat16)
    result = lax.map(one_block, (u_blocks, v_blocks))
    return result.reshape(whole_u.shape[0], whole_u.shape[0], 2, whole_u.shape[3])
```

```python
import functools
import math

import jax
import jax.numpy as jnp
from jax import lax
from jax.experimental import pallas as pl
from jax.experimental.pallas import tpu as pltpu
from jax.sharding import PartitionSpec as P

WIN_LEN = 1000
GROUP = 128
REACH = 64


def normalize(strain):
    width = 2 * REACH + 1
    magnitude = jnp.abs(strain)
    zero_val = jnp.zeros((), magnitude.dtype)
    running = lax.reduce_window(
        magnitude, zero_val, lax.add, (1, 1, width), (1, 1, 1), ((0, 0), (0, 0), (REACH, REACH))
    )
    unit_row = jnp.ones((strain.shape[2],), magnitude.dtype)
    counts = lax.reduce_window(unit_row, zero_val, lax.add, (width,), (1,), ((REACH, REACH),))
    return strain / (running / counts + 1e-06)


def cut_windows(normed, offsets):

    def one_file(rows, starts):
        return jax.vmap(lambda start_pos: lax.dynamic_slice_in_dim(rows, start_pos, WIN_LEN, 1))(
            starts
        )

    pieces = jax.vmap(one_file, in_axes=(1, 0))(normed, offsets)
    sample_pos = jnp.arange(WIN_LEN, dtype=jnp.float32)
    hann_taper = 0.5 - 0.5 * jnp.cos(2.0 * math.pi * (sample_pos + 0.5) / WIN_LEN)
    return (jnp.transpose(pieces, (2, 0, 1, 3)) * hann_taper).astype(jnp.bfloat16)


def make_table(bins):
    sample_idx = jnp.arange(WIN_LEN, dtype=jnp.int32)
    phase_idx = sample_idx[:, None] * bins[None, :] % WIN_LEN
    angles = phase_idx.astype(jnp.float32) * (2.0 * math.pi / WIN_LEN)
    return jnp.concatenate([jnp.cos(angles), -jnp.sin(angles)], axis=1).astype(jnp.bfloat16)


def spectra(windows, table):
    flat_rows = windows.reshape(-1, WIN_LEN)
    result = jnp.dot(flat_rows, table, preferred_element_type=jnp.float32)
    return result.reshape(
        windows.shape[0], windows.shape[1] * windows.shape[2], 2, table.shape[1] // 2
    )


def whiten(spec):
    chan_rows, win_count, _, bin_count = spec.shape
    grouped = spec.reshape(chan_rows, win_count, 2, bin_count // GROUP, GROUP)
    power_mean = jnp.mean(jnp.sum(grouped * grouped, axis=2), axis=-1, keepdims=True)
    gain_inv = lax.rsqrt(power_mean + 1e-06)[:, :, None]
    return (grouped * gain_inv).reshape(spec.shape).astype(jnp.bfloat16)


def cross_block(lhs_rows, other, win_count):
    products = jnp.einsum("iwcf,jwcf->ijf", lhs_rows, other, preferred_element_type=jnp.float32)
    chan_rows = lhs_rows.shape[0] // 2
    split_parts = products.reshape(2, chan_rows, other.shape[0], products.shape[2])
    return (jnp.transpose(split_parts, (1, 2, 0, 3)) / win_count).astype(jnp.bfloat16)


def on_any(strain, offsets, bins):
    normed = normalize(strain)
    windows = cut_windows(normed, offsets)
    band_count = lax.axis_size("band")
    bin_share = bins.shape[0] // band_count
    all_windows = lax.all_gather(windows, "band", axis=1, tiled=True)
    my_bins = lax.dynamic_slice_in_dim(bins, lax.axis_index("band") * bin_share, bin_share)
    whitened = whiten(spectra(all_windows, make_table(my_bins)))
    chan_rows = whitened.shape[0]
    win_count = whitened.shape[1]
    rotated = jnp.stack([whitened[:, :, 1], -whitened[:, :, 0]], axis=2)
    lhs_rows = jnp.concatenate([whitened, rotated], axis=0)
    chan_count = lax.axis_size("chan")
    col_count = chan_rows * chan_count
    blank_out = jnp.zeros((chan_rows, col_count, 2, bin_share), jnp.bfloat16)
    return lax.dynamic_update_slice_in_dim(
        blank_out,
        cross_block(lhs_rows, lax.all_gather(whitened, "chan", axis=0, tiled=True), win_count),
        jnp.int32(0),
        1,
    )


def round_up(size, step):
    return -(-size // step) * step


def spectra_kernel(samples, win_file, depth, offs_ref, strain_ref, hann_ref, table_ref, out_ref, mags, normed):
    m = pl.program_id(0)
    rows = mags.shape[0]
    chans = mags.shape[1]
    mags[pl.ds(0, REACH), :] = jnp.zeros((REACH, chans), jnp.float32)
    mags[pl.ds(REACH, samples), :] = jnp.abs(strain_ref[0])
    mags[pl.ds(REACH + samples, rows - REACH - samples), :] = jnp.zeros(
        (rows - REACH - samples, chans), jnp.float32
    )
    first = mags[...]
    total = first
    reach = 1
    while reach < 2 * REACH:
        total = total + pltpu.roll(total, rows - reach, 0)
        reach *= 2
    total = (total + pltpu.roll(first, rows - reach, 0))[:samples]
    pos = lax.broadcasted_iota(jnp.int32, (samples, chans), 0)
    counts = jnp.minimum(pos + REACH, samples - 1) - jnp.maximum(pos - REACH, 0) + 1
    normed[pl.ds(0, samples), :] = strain_ref[0] / (total / counts.astype(jnp.float32) + 1e-06)
    spare = normed.shape[0] - samples
    normed[pl.ds(samples, spare), :] = jnp.zeros((spare, chans), jnp.float32)
    for k in range(win_file):
        window = (normed[pl.ds(offs_ref[m, k], depth), :] * hann_ref[...]).astype(jnp.bfloat16)
        spec = jnp.dot(table_ref[...], window, preferred_element_type=jnp.float32)
        for g in range(spec.shape[0] // (2 * GROUP)):
            part = spec[g * 2 * GROUP : (g + 1) * 2 * GROUP]
            power = jnp.sum(part * part, axis=0, keepdims=True) / GROUP
            out_ref[k, pl.ds(g * 2 * GROUP, 2 * GROUP), :] = (
                part * lax.rsqrt(power + 1e-06)
            ).astype(jnp.bfloat16)


def own_spectra(strain, offsets, bins):
    chans, files, samples = strain.shape
    win_file = offsets.shape[1]
    depth = round_up(WIN_LEN, 128)
    table = make_table(bins)
    parts = table.reshape(WIN_LEN, 2, bins.shape[0] // GROUP, GROUP)
    rows = jnp.transpose(parts, (2, 1, 3, 0)).reshape(2 * bins.shape[0], WIN_LEN)
    rows = jnp.pad(rows, ((0, 0), (0, depth - WIN_LEN)))
    sample_pos = jnp.arange(WIN_LEN, dtype=jnp.float32)
    taper = 0.5 - 0.5 * jnp.cos(2.0 * math.pi * (sample_pos + 0.5) / WIN_LEN)
    taper = jnp.broadcast_to(jnp.pad(taper, (0, depth - WIN_LEN))[:, None], (depth, chans))
    return pl.pallas_call(
        functools.partial(spectra_kernel, samples, win_file, depth),
        grid_spec=pltpu.PrefetchScalarGridSpec(
            num_scalar_prefetch=1,
            grid=(files,),
            in_specs=[
                pl.BlockSpec((1, samples, chans), lambda m, o: (m, 0, 0)),
                pl.BlockSpec((depth, chans), lambda m, o: (0, 0)),
                pl.BlockSpec((2 * bins.shape[0], depth), lambda m, o: (0, 0)),
            ],
            out_specs=pl.BlockSpec((win_file, 2 * bins.shape[0], chans), lambda m, o: (m, 0, 0)),
            scratch_shapes=[
                pltpu.VMEM((round_up(samples + 2 * REACH, 8), chans), jnp.float32),
                pltpu.VMEM((round_up(samples - WIN_LEN + depth, 8), chans), jnp.float32),
            ],
        ),
        out_shape=jax.ShapeDtypeStruct(
            (files * win_file, 2 * bins.shape[0], chans), jnp.bfloat16
        ),
        compiler_params=pltpu.CompilerParams(vmem_limit_bytes=40 * 2**20),
        name="spectra",
    )(offsets, jnp.transpose(strain, (1, 2, 0)), taper, rows)


FSTEP = 8
ISTEP = 16


def cross_kernel(win_count, slot_ref, lhs_ref, rhs_ref, place_ref, prior_ref, out_ref, low, high):
    bins, chans, depth = lhs_ref.shape
    half = depth // 2

    @pl.when(pl.program_id(0) == 0)
    def _():
        @pl.loop(0, bins // FSTEP)
        def _(step):
            base = step * FSTEP
            block = rhs_ref[pl.ds(base, FSTEP)]
            turned = jnp.concatenate([-block[:, half:], block[:, :half]], axis=1)
            both = jnp.concatenate([block, turned], axis=2).reshape(FSTEP * depth, 2 * chans)
            mixed = jnp.dot(both, place_ref[...], preferred_element_type=jnp.float32)
            mixed = mixed.astype(jnp.bfloat16).reshape(FSTEP, depth, 2 * chans)
            for q in range(FSTEP):
                prod = jnp.dot(lhs_ref[base + q], mixed[q], preferred_element_type=jnp.float32)
                prod = prod / win_count
                at = pl.ds(pl.multiple_of((base + q) * chans, chans), chans)
                low[at, :] = prod[:, :chans]
                high[at, :] = prod[:, chans:]

    first = pl.program_id(0) * ISTEP
    for q in range(ISTEP):
        at = pl.ds(first + q, bins, stride=chans)
        out_ref[q, pl.ds(0, chans), :] = low[at, :].T.astype(jnp.bfloat16)
        out_ref[q, pl.ds(chans, chans), :] = high[at, :].T.astype(jnp.bfloat16)


def cross_slot(lhs, rhs, place, prior, slot, blocks, win_count):
    bins, chans, depth = lhs.shape
    shape = jax.ShapeDtypeStruct((chans, 2 * chans * blocks, bins), jnp.bfloat16)
    body = functools.partial(cross_kernel, win_count)
    in_specs = [
        pl.BlockSpec((bins, chans, depth), lambda i, s: (0, 0, 0)),
        pl.BlockSpec((bins, depth, chans), lambda i, s: (0, 0, 0)),
        pl.BlockSpec((2 * chans, 2 * chans), lambda i, s: (0, 0)),
    ]
    operands = [slot, lhs, rhs, place]
    aliases = {}
    if prior is None:
        def body(slot_ref, lhs_ref, rhs_ref, place_ref, *rest):
            cross_kernel(win_count, slot_ref, lhs_ref, rhs_ref, place_ref, None, *rest)
    else:
        in_specs.append(pl.BlockSpec(memory_space=pl.ANY))
        operands.append(prior)
        aliases = {4: 0}
    return pl.pallas_call(
        body,
        grid_spec=pltpu.PrefetchScalarGridSpec(
            num_scalar_prefetch=1,
            grid=(chans // ISTEP,),
            in_specs=in_specs,
            out_specs=pl.BlockSpec((ISTEP, 2 * chans, bins), lambda i, s: (i, s[0], 0)),
            scratch_shapes=[pltpu.VMEM((bins * chans, chans), jnp.float32)] * 2,
        ),
        out_shape=shape,
        input_output_aliases=aliases,
        compiler_params=pltpu.CompilerParams(vmem_limit_bytes=48 * 2**20),
        cost_estimate=pl.CostEstimate(
            flops=4 * bins * depth * chans * chans,
            bytes_accessed=30 * 2**20,
            transcendentals=0,
        ),
        name="cross",
    )(*operands)


def own_bins(strain, offsets, bins):
    band_count = lax.axis_size("band")
    me = lax.axis_index("band")
    mine = own_spectra(strain, offsets, bins)
    win_count, _, chans = mine.shape
    mine = mine.reshape(win_count, band_count, -1, 2, GROUP, chans)
    pieces = [lax.dynamic_index_in_dim(mine, me, 1, False)]
    for hop in range(1, band_count):
        sent = lax.dynamic_index_in_dim(mine, (me + hop) % band_count, 1, False)
        pieces.append(
            lax.ppermute(sent, "band", [(b, (b + hop) % band_count) for b in range(band_count)])
        )
    joined = jnp.stack(pieces)
    turned = jnp.transpose(joined, (2, 4, 3, 0, 1, 5))
    return turned.reshape(bins.shape[0] // band_count, 2 * band_count * win_count, chans)


def on_line(strain, offsets, bins):
    block = own_bins(strain, offsets, bins)
    bin_share, depth, chans = block.shape
    lhs = jnp.transpose(block, (0, 2, 1))
    spot = jnp.arange(2 * chans)
    place = (spot[None, :] == (2 * (spot % chans) + spot // chans)[:, None]).astype(jnp.bfloat16)
    me = lax.axis_index("chan")
    z, x = me // 2, me % 2

    def along(value, step, reach):
        ends = [(a, a + step) for a in range(4) if 0 <= a + step < 4 and 0 <= a - (reach - 1) * step < 4]
        return lax.ppermute(value, "chan", [(2 * a + s, 2 * b + s) for a, b in ends for s in range(2)])

    def across(value):
        return lax.ppermute(value, "chan", [(c, c ^ 1) for c in range(8)])

    def cross(value, number, prior):
        return cross_slot(lhs, value, place, prior, number.astype(jnp.int32).reshape(1), 8, depth // 2)

    near_z = jnp.where(z > 0, z - 1, z + 1)
    mid_z = jnp.where(z >= 2, z - 2, z + 2)
    last_z = jnp.where(z == 0, 3, jnp.where(z == 3, 0, z + 1))

    up1, down1, other = along(block, 1, 1), along(block, -1, 1), across(block)
    out = cross(block, me, None)
    up1, down1, out = lax.optimization_barrier((up1, down1, out))

    near = jnp.where(z > 0, up1, down1)
    up2, down2, near_other = along(up1, 1, 2), along(down1, -1, 2), across(near)
    out = cross(other, 2 * z + 1 - x, out)
    out = cross(near, 2 * near_z + x, out)
    up2, down2, out = lax.optimization_barrier((up2, down2, out))

    mid = jnp.where(z >= 2, up2, down2)
    up3, down3, mid_other = along(mid, 1, 3), along(mid, -1, 3), across(mid)
    out = cross(near_other, 2 * near_z + 1 - x, out)
    out = cross(mid, 2 * mid_z + x, out)
    up3, down3, out = lax.optimization_barrier((up3, down3, out))

    last = jnp.where(z == 0, down3, jnp.where(z == 3, up3, down1))
    last_other = across(last)
    out = cross(mid_other, 2 * mid_z + 1 - x, out)
    out = cross(last, 2 * last_z + x, out)
    out = cross(last_other, 2 * last_z + 1 - x, out)
    return out.reshape(chans, 8 * chans, 2, bin_share)


def on_device(strain, offsets, bins):
    if strain.shape[0] == 128 and lax.axis_size("chan") == 8 and bins.shape[0] // lax.axis_size("band") == 128:
        return on_line(strain, offsets, bins)
    return on_any(strain, offsets, bins)


def solution(mesh):
    placed = (P(("seg", "chan"), "band", None), P(("seg", "band"), None), P())
    return jax.shard_map(
        on_device,
        mesh=mesh,
        in_specs=placed,
        out_specs=P(("seg", "chan"), None, None, "band"),
        check_vma=False,
    )
```
